128 devices in a mesh: rows: 32 (over z, x, core), rep: 4 (over y).
Axes of the slice: x: 4, y: 4, z: 4, core: 2. Of those that a mesh axis runs over, the one named last changes fastest.
Arguments:
- features: bfloat16 [65536, 512], P(('rows', 'rep')), may hold values from -6 to 6
- weight: bfloat16 [512, 512], replicated, may hold values from -6 to 6
- out_bias: float32 [512], replicated, may hold values from -4 to 4
- degree: int32 [65536], P(('rows', 'rep')), may hold values from 256 to 1023
- tile_row: int32 [8192], P(('rows', 'rep')), may hold values from 0 to 15, as said below
- tile_col: int32 [8192], P(('rows', 'rep')), may hold values from 0 to 127, as said below
- tile_value: bfloat16 [8192, 128, 128], P(('rows', 'rep')), may hold values from 0 to 3, as said below
- cotangent: bfloat16 [65536, 512], P(('rows', 'rep')), may hold values from -6 to 6
Outputs:
- hidden_out: bfloat16 [65536, 512], P(('rows', 'rep'))
- grad_input: bfloat16 [65536, 512], P(('rows', 'rep'))
- grad_weight: float32 [512, 512], replicated
The draws below stay inside these ranges and needn't reach their ends.
Inputs may be any that keep to these rules, and one draw needn't show every extreme that they name: `tile_row`: on each device the slots that hold edges come first; every later slot has an all-zero tile and both of its indices 0. Every node block's diagonal block is among its device's slots. Columns of a device's group are numbered slab by slab: tile_col = j * 4 + b names node block (j * 4 + c) * 4 + b. `tile_value`: all slots together form a symmetric adjacency: for every slot with tile V on global blocks (g, h) there is a slot on (h, g) with tile V transposed, and a diagonal block's tile is symmetric. Entries are 0 or between 0.1 and 3.
All inputs are finite; a program needn't handle non-finite values.
Results may differ from the reference program's by a relative error of at most 0.0061.
Values may be sent and summed in bfloat16 or wider, within the bound.
A program may use at most 128 MiB of HBM per device.

```python
import jax
import jax.numpy as jnp
from jax import lax

F = 512
TILE = 128
LINKS = 15
BLOCKS_DEV = 4
SLOTS = 64
NODES = 65536
N_ROWS = 32
N_REP = 4


def layout(key):
    base_key = jax.random.fold_in(key, 911)
    mask_key, level_key, hub_key = jax.random.split(base_key, 3)
    total_blocks = BLOCKS_DEV * N_ROWS * N_REP
    devices = N_ROWS * N_REP
    link_masks = jax.random.randint(mask_key, (LINKS,), 1, total_blocks, dtype=jnp.int32)
    link_masks = link_masks.at[0].set(BLOCKS_DEV * N_REP)
    levels = jax.random.randint(level_key, (total_blocks,), 0, LINKS // 2 + 1, dtype=jnp.int32)
    hub_slab = jax.random.randint(hub_key, (), 0, N_ROWS, dtype=jnp.int32)
    slab_index = jnp.arange(total_blocks, dtype=jnp.int32) // (BLOCKS_DEV * N_REP)
    levels = jnp.where(slab_index == hub_slab, LINKS, levels)
    device = jnp.arange(devices, dtype=jnp.int32)[:, None, None]
    row_slab = device // N_REP
    column_group = device % N_REP
    link_index = jnp.arange(LINKS + 1, dtype=jnp.int32)[None, :, None]
    within = jnp.arange(BLOCKS_DEV, dtype=jnp.int32)[None, None, :]
    masks_all = jnp.concatenate([link_masks, jnp.zeros((1,), jnp.int32)])[link_index]
    group_flip = masks_all // BLOCKS_DEV % N_REP
    source_group = jnp.bitwise_xor(column_group, group_flip)
    full_shape = (devices, LINKS + 1, BLOCKS_DEV)
    row_block = jnp.broadcast_to((row_slab * N_REP + source_group) * BLOCKS_DEV + within, full_shape)
    col_block = jnp.bitwise_xor(row_block, jnp.broadcast_to(masks_all, full_shape))
    link_full = jnp.broadcast_to(link_index, full_shape)
    is_live = (link_full == LINKS) | (link_full == 0) | (link_full < levels[row_block] + levels[col_block])
    local_row = jnp.broadcast_to(source_group * BLOCKS_DEV + within, full_shape)
    local_col = col_block // (BLOCKS_DEV * N_REP) * BLOCKS_DEV + col_block % BLOCKS_DEV
    ranking = jnp.where(is_live, 0, SLOTS).reshape(devices, SLOTS) + jnp.arange(SLOTS, dtype=jnp.int32)[None, :]
    ordering = jnp.argsort(ranking, axis=1)

    def reorder(values):
        return jnp.take_along_axis(values.reshape(devices, SLOTS), ordering, axis=1).reshape(-1)
    return (reorder(is_live), reorder(local_row), reorder(local_col), reorder(row_block), reorder(col_block), reorder(link_full))


def draw_tile_row(key, part):
    is_live, local_row, local_col, row_block, col_block, link_full = layout(key)
    return jnp.where(is_live, local_row, 0).astype(jnp.int32)


def draw_tile_col(key, part):
    is_live, local_row, local_col, row_block, col_block, link_full = layout(key)
    return jnp.where(is_live, local_col, 0).astype(jnp.int32)


def draw_tile_value(key, part):
    is_live, local_row, local_col, row_block, col_block, link_full = layout(key)
    value_key = jax.random.fold_in(key, 433)
    upper = jnp.arange(TILE)[:, None] <= jnp.arange(TILE)[None, :]

    def one_tile(row_b, col_b, link_b, live_b):
        lower_id = jnp.minimum(row_b, col_b)
        higher_id = jnp.maximum(row_b, col_b)
        tile_key = jax.random.fold_in(jax.random.fold_in(jax.random.fold_in(value_key, link_b), lower_id), higher_id)
        present_key, weight_key = jax.random.split(tile_key)
        present = jax.random.bernoulli(present_key, 0.25, (TILE, TILE))
        weights = jax.random.uniform(weight_key, (TILE, TILE), jnp.float32, 0.5, 1.5)
        raw_tile = jnp.where(present, weights, 0.0)
        turned = jnp.where(row_b > col_b, raw_tile.T, raw_tile)
        mirrored = jnp.where(upper, raw_tile, raw_tile.T)
        result = jnp.where(row_b == col_b, mirrored, turned)
        return jnp.where(live_b, result, 0.0)
    values = jax.vmap(one_tile)(row_block, col_block, link_full, is_live)
    return values.astype(jnp.bfloat16)


def touch_ends(values, rng, smallest, high):
    dims = values.shape
    place = [jax.random.randint(jax.random.fold_in(rng, axis), (), 0, dims[axis]) for axis in range(len(dims))]
    values = values.at[tuple(place)].set(smallest)
    longest = dims.index(max(dims))
    place[longest] = (place[longest] + 1) % dims[longest]
    return values.at[tuple(place)].set(high)


def shard_levels(rng, shape, cuts, smallest, high):
    gain, own = 1.0, jax.random.fold_in(rng, 6)
    for dim, parts in cuts:
        steps = jnp.exp(jax.random.uniform(jax.random.fold_in(own, dim), (parts,), jnp.float32, smallest / len(cuts), high / len(cuts)))
        gain = gain * jnp.repeat(steps, shape[dim] // parts).reshape([-1 if axis == dim else 1 for axis in range(len(shape))])
    return gain


def centred(rng, shape, deviation, bound, cuts=(), kind=jnp.bfloat16):
    drawn = deviation * jax.random.normal(rng, shape, jnp.float32)
    if cuts:
        drawn = drawn * shard_levels(rng, shape, cuts, -0.22, 0.18)
    return jnp.clip(drawn, -bound, bound).astype(kind)


def setup_inputs(seed: int = 0) -> dict:
    key_list = jax.random.split(jax.random.key(seed), 9)
    return {
        "features": centred(key_list[0], (NODES, F), 1.0, 6.0, ((0, 128),)),
        "weight": centred(key_list[1], (F, F), (F * 4 // ((LINKS + 1) * TILE)) ** -0.5, 6.0),
        "out_bias": centred(key_list[2], (F,), 1.0, 4.0, (), jnp.float32),
        "degree": touch_ends(jax.random.randint(key_list[3], (NODES,), (LINKS + 1) * TILE // 8, (LINKS + 1) * TILE // 2), jax.random.fold_in(key_list[3], 1), (LINKS + 1) * TILE // 8, ((LINKS + 1) * TILE // 2) - 1).astype(jnp.int32),
        "tile_row": draw_tile_row(jax.random.fold_in(key_list[8], 71), 0),
        "tile_col": draw_tile_col(jax.random.fold_in(key_list[8], 71), 0),
        "tile_value": draw_tile_value(jax.random.fold_in(key_list[8], 71), 0),
        "cotangent": centred(key_list[7], (NODES, F), 1.0, 6.0, ((0, 128),)),
    }


def spread(source, tiles_all, from_index, to_index, flipped, total_blocks):
    feat_width = source.shape[1]
    devices = N_ROWS * N_REP
    panel_blocks = source.reshape(total_blocks, TILE, feat_width).astype(jnp.float32)

    def per_device(totals, bundle):
        tiles, src_idx, dst_idx = bundle
        tiles = tiles.astype(jnp.float32)
        if flipped:
            products = jnp.einsum('sji,sjf->sif', tiles, panel_blocks[src_idx])
        else:
            products = jnp.einsum('sij,sjf->sif', tiles, panel_blocks[src_idx])
        return (totals.at[dst_idx].add(products), None)
    initial = jnp.zeros((total_blocks, TILE, feat_width), jnp.float32)
    bundles = (tiles_all.reshape(devices, SLOTS, TILE, TILE), from_index.reshape(devices, SLOTS), to_index.reshape(devices, SLOTS))
    totals, _ = lax.scan(per_device, initial, bundles)
    return totals.reshape(total_blocks * TILE, feat_width)

def reference(features, weight, out_bias, degree, tile_row, tile_col, tile_value, cotangent):
    total_blocks = features.shape[0] // TILE
    devices = N_ROWS * N_REP
    row_scale = lax.rsqrt(degree.astype(jnp.float32))[:, None]
    scaled = (jnp.dot(features, weight, preferred_element_type=jnp.float32) * row_scale).astype(jnp.bfloat16)
    slot_device = jnp.arange(devices * SLOTS, dtype=jnp.int32) // SLOTS
    row_slab = slot_device // N_REP
    column_group = slot_device % N_REP
    global_row = (row_slab * (N_REP * BLOCKS_DEV) + tile_row).astype(jnp.int32)
    global_col = ((tile_col // BLOCKS_DEV * N_REP + column_group) * BLOCKS_DEV + tile_col % BLOCKS_DEV).astype(jnp.int32)
    aggregate = spread(scaled, tile_value, global_col, global_row, False, total_blocks) * row_scale
    pre_act = aggregate + out_bias
    hidden_out = jax.nn.silu(pre_act).astype(jnp.bfloat16)
    sigmoid_pre = jax.nn.sigmoid(pre_act)
    grad_pre = cotangent.astype(jnp.float32) * sigmoid_pre * (1.0 + pre_act * (1.0 - sigmoid_pre))
    scaled_grad = (grad_pre * row_scale).astype(jnp.bfloat16)
    back_sum = (spread(scaled_grad, tile_value, global_row, global_col, True, total_blocks) * row_scale).astype(jnp.bfloat16)
    grad_input = jnp.dot(back_sum, weight.T, preferred_element_type=jnp.float32).astype(jnp.bfloat16)
    grad_weight = jnp.dot(features.T, back_sum, preferred_element_type=jnp.float32)
    return (hidden_out, grad_input, grad_weight)
```

```python
import jax
import jax.numpy as jnp
from jax import lax
from jax.experimental import pallas as pl
from jax.experimental.pallas import tpu as pltpu
from jax.sharding import PartitionSpec as P


def _aggregate_kernel(rows_ref, cols_ref, tile_ref, panel_ref, out_ref):
    s = pl.program_id(0)

    @pl.when(s == 0)
    def _():
        out_ref[...] = jnp.zeros_like(out_ref)

    tile_size = tile_ref.shape[1]
    start = pl.multiple_of(rows_ref[s] * tile_size, tile_size)
    product = jnp.dot(tile_ref[0], panel_ref[...], preferred_element_type=jnp.float32)
    out_ref[pl.ds(start, tile_size), :] += product


def aggregate_slots(panels, group_rows, group_cols, tiles, out_blocks):
    slot_count, tile_size, _ = tiles.shape
    feat_width = panels.shape[1]
    grid_spec = pltpu.PrefetchScalarGridSpec(
        num_scalar_prefetch=2,
        grid=(slot_count,),
        in_specs=[
            pl.BlockSpec((1, tile_size, tile_size), lambda s, rows, cols: (s, 0, 0)),
            pl.BlockSpec((tile_size, feat_width), lambda s, rows, cols: (cols[s], 0)),
        ],
        out_specs=pl.BlockSpec((out_blocks * tile_size, feat_width), lambda s, rows, cols: (0, 0)),
    )
    return pl.pallas_call(
        _aggregate_kernel,
        grid_spec=grid_spec,
        out_shape=jax.ShapeDtypeStruct((out_blocks * tile_size, feat_width), jnp.float32),
        compiler_params=pltpu.CompilerParams(dimension_semantics=("arbitrary",)),
    )(group_rows, group_cols, tiles, panels)


def shards(features, weight, out_bias, degree, tile_row, tile_col, tile_value, cotangent):
    tile_size = tile_value.shape[1]
    nodes_dev = features.shape[0]
    block_count = nodes_dev // tile_size
    rep_count = lax.axis_size("rep")
    row_scale = lax.rsqrt(degree.astype(jnp.float32))[:, None]
    scaled = (jnp.dot(features, weight, preferred_element_type=jnp.float32) * row_scale).astype(
        jnp.bfloat16
    )
    panels = lax.all_gather(scaled, "rows", axis=0, tiled=True)
    slab_part = aggregate_slots(panels, tile_row, tile_col, tile_value, rep_count * block_count)
    aggregate = lax.psum_scatter(slab_part, "rep", scatter_dimension=0, tiled=True) * row_scale
    pre_act = aggregate + out_bias
    hidden_out = jax.nn.silu(pre_act).astype(jnp.bfloat16)
    sigmoid_pre = jax.nn.sigmoid(pre_act)
    grad_pre = cotangent.astype(jnp.float32) * sigmoid_pre * (1.0 + pre_act * (1.0 - sigmoid_pre))
    scaled_grad = (grad_pre * row_scale).astype(jnp.bfloat16)
    grad_panels = lax.all_gather(scaled_grad, "rows", axis=0, tiled=True)
    back_part = aggregate_slots(grad_panels, tile_row, tile_col, tile_value, rep_count * block_count)
    back_total = lax.psum_scatter(back_part, "rep", scatter_dimension=0, tiled=True)
    back_sum = (back_total * row_scale).astype(jnp.bfloat16)
    grad_input = lax.dot_general(
        back_sum, weight, (((1,), (1,)), ((), ())), preferred_element_type=jnp.float32
    ).astype(jnp.bfloat16)
    local_weight = lax.dot_general(
        features, back_sum, (((0,), (0,)), ((), ())), preferred_element_type=jnp.float32
    )
    grad_weight = lax.psum(local_weight, ("rows", "rep"))
    return (hidden_out, grad_input, grad_weight)


def solution(mesh):
    placed = (
        P(("rows", "rep"), None),
        P(),
        P(),
        P(("rows", "rep")),
        P(("rows", "rep")),
        P(("rows", "rep")),
        P(("rows", "rep"), None, None),
        P(("rows", "rep"), None),
    )
    return jax.shard_map(
        shards,
        mesh=mesh,
        in_specs=placed,
        out_specs=(P(("rows", "rep"), None), P(("rows", "rep"), None), P()),
        check_vma=False,
    )
```

```python
import jax
import jax.numpy as jnp
from jax import lax
from jax.experimental import pallas as pl
from jax.experimental.pallas import tpu as pltpu
from jax.sharding import PartitionSpec as P


def _aggregate_kernel(rows_ref, cols_ref, tile_ref, panel_ref, out_ref):
    s = pl.program_id(0)

    @pl.when(s == 0)
    def _():
        out_ref[...] = jnp.zeros_like(out_ref)

    tile_size = tile_ref.shape[1]
    start = pl.multiple_of(rows_ref[s] * tile_size, tile_size)
    product = jnp.dot(tile_ref[0], panel_ref[...], preferred_element_type=jnp.float32)
    out_ref[pl.ds(start, tile_size), :] += product


def aggregate_slots(panels, group_rows, group_cols, tiles, out_blocks):
    slot_count, tile_size, _ = tiles.shape
    feat_width = panels.shape[1]
    grid_spec = pltpu.PrefetchScalarGridSpec(
        num_scalar_prefetch=2,
        grid=(slot_count,),
        in_specs=[
            pl.BlockSpec((1, tile_size, tile_size), lambda s, rows, cols: (s, 0, 0)),
            pl.BlockSpec((tile_size, feat_width), lambda s, rows, cols: (cols[s], 0)),
        ],
        out_specs=pl.BlockSpec((out_blocks * tile_size, feat_width), lambda s, rows, cols: (0, 0)),
    )
    return pl.pallas_call(
        _aggregate_kernel,
        grid_spec=grid_spec,
        out_shape=jax.ShapeDtypeStruct((out_blocks * tile_size, feat_width), jnp.float32),
        compiler_params=pltpu.CompilerParams(dimension_semantics=("arbitrary",)),
    )(group_rows, group_cols, tiles, panels)


def all_reduce_by_exchange(value, axes):
    count = 1
    for axis in axes:
        count *= lax.axis_size(axis)
    rows, width = value.shape
    chunks = lax.all_to_all(value.reshape(count, rows // count, width), axes, 0, 0, tiled=True)
    own = chunks.sum(axis=0)
    spread = jnp.broadcast_to(own[None], (count,) + own.shape)
    return lax.all_to_all(spread, axes, 0, 0, tiled=True).reshape(rows, width)


def shards(features, weight, out_bias, degree, tile_row, tile_col, tile_value, cotangent):
    tile_size = tile_value.shape[1]
    nodes_dev = features.shape[0]
    block_count = nodes_dev // tile_size
    rep_count = lax.axis_size("rep")
    row_scale = lax.rsqrt(degree.astype(jnp.float32))[:, None]
    scaled = (jnp.dot(features, weight, preferred_element_type=jnp.float32) * row_scale).astype(
        jnp.bfloat16
    )
    panels = lax.all_gather(scaled, "rows", axis=0, tiled=True)
    slab_part = aggregate_slots(panels, tile_row, tile_col, tile_value, rep_count * block_count)
    aggregate = lax.psum_scatter(slab_part, "rep", scatter_dimension=0, tiled=True) * row_scale
    pre_act = aggregate + out_bias
    hidden_out = jax.nn.silu(pre_act).astype(jnp.bfloat16)
    sigmoid_pre = jax.nn.sigmoid(pre_act)
    grad_pre = cotangent.astype(jnp.float32) * sigmoid_pre * (1.0 + pre_act * (1.0 - sigmoid_pre))
    scaled_grad = (grad_pre * row_scale).astype(jnp.bfloat16)
    grad_panels = lax.all_gather(scaled_grad, "rows", axis=0, tiled=True)
    back_part = aggregate_slots(grad_panels, tile_row, tile_col, tile_value, rep_count * block_count)
    back_total = lax.psum_scatter(back_part, "rep", scatter_dimension=0, tiled=True)
    back_sum = (back_total * row_scale).astype(jnp.bfloat16)
    grad_input = lax.dot_general(
        back_sum, weight, (((1,), (1,)), ((), ())), preferred_element_type=jnp.float32
    ).astype(jnp.bfloat16)
    local_weight = lax.dot_general(
        features, back_sum, (((0,), (0,)), ((), ())), preferred_element_type=jnp.float32
    )
    grad_weight = all_reduce_by_exchange(local_weight, ("rows", "rep"))
    return (hidden_out, grad_input, grad_weight)


def solution(mesh):
    placed = (
        P(("rows", "rep"), None),
        P(),
        P(),
        P(("rows", "rep")),
        P(("rows", "rep")),
        P(("rows", "rep")),
        P(("rows", "rep"), None, None),
        P(("rows", "rep"), None),
    )
    return jax.shard_map(
        shards,
        mesh=mesh,
        in_specs=placed,
        out_specs=(P(("rows", "rep"), None), P(("rows", "rep"), None), P()),
        check_vma=False,
    )
```

```python
import jax
import jax.numpy as jnp
from jax import lax
from jax.experimental import pallas as pl
from jax.experimental.pallas import tpu as pltpu
from jax.sharding import PartitionSpec as P


def _aggregate_kernel(rows_ref, cols_ref, tile_ref, panel_ref, out_ref):
    s = pl.program_id(0)

    @pl.when(s == 0)
    def _():
        out_ref[...] = jnp.zeros_like(out_ref)

    tile_size = tile_ref.shape[1]
    start = pl.multiple_of(rows_ref[s] * tile_size, tile_size)
    product = jnp.dot(tile_ref[0], panel_ref[...], preferred_element_type=jnp.float32)
    out_ref[pl.ds(start, tile_size), :] += product


def aggregate_slots(panels, group_rows, group_cols, tiles, out_blocks):
    slot_count, tile_size, _ = tiles.shape
    feat_width = panels.shape[1]
    grid_spec = pltpu.PrefetchScalarGridSpec(
        num_scalar_prefetch=2,
        grid=(slot_count,),
        in_specs=[
            pl.BlockSpec((1, tile_size, tile_size), lambda s, rows, cols: (s, 0, 0)),
            pl.BlockSpec((tile_size, feat_width), lambda s, rows, cols: (cols[s], 0)),
        ],
        out_specs=pl.BlockSpec((out_blocks * tile_size, feat_width), lambda s, rows, cols: (0, 0)),
    )
    return pl.pallas_call(
        _aggregate_kernel,
        grid_spec=grid_spec,
        out_shape=jax.ShapeDtypeStruct((out_blocks * tile_size, feat_width), jnp.float32),
        compiler_params=pltpu.CompilerParams(dimension_semantics=("arbitrary",)),
    )(group_rows, group_cols, tiles, panels)


def all_reduce_by_exchange(value, axes):
    count = 1
    for axis in axes:
        count *= lax.axis_size(axis)
    rows, width = value.shape
    chunks = lax.all_to_all(value.reshape(count, rows // count, width), axes, 0, 0, tiled=True)
    own = chunks.sum(axis=0)
    spread = jnp.broadcast_to(own[None], (count,) + own.shape)
    return lax.all_to_all(spread, axes, 0, 0, tiled=True).reshape(rows, width)


COLUMN_CHUNKS = 2


def shards(features, weight, out_bias, degree, tile_row, tile_col, tile_value, cotangent):
    tile_size = tile_value.shape[1]
    nodes_dev = features.shape[0]
    feat_width = weight.shape[1]
    block_count = nodes_dev // tile_size
    rep_count = lax.axis_size("rep")
    width = feat_width // COLUMN_CHUNKS
    row_scale = lax.rsqrt(degree.astype(jnp.float32))[:, None]
    scaled = (jnp.dot(features, weight, preferred_element_type=jnp.float32) * row_scale).astype(
        jnp.bfloat16
    )
    hidden_parts, weight_parts = [], []
    grad_input = None
    for k in range(COLUMN_CHUNKS):
        cols = slice(k * width, (k + 1) * width)
        panels = lax.all_gather(scaled[:, cols], "rows", axis=0, tiled=True)
        slab_part = aggregate_slots(panels, tile_row, tile_col, tile_value, rep_count * block_count)
        aggregate = lax.psum_scatter(slab_part, "rep", scatter_dimension=0, tiled=True) * row_scale
        pre_act = aggregate + out_bias[cols]
        hidden_parts.append(jax.nn.silu(pre_act).astype(jnp.bfloat16))
        sigmoid_pre = jax.nn.sigmoid(pre_act)
        grad_pre = cotangent[:, cols].astype(jnp.float32) * sigmoid_pre * (
            1.0 + pre_act * (1.0 - sigmoid_pre)
        )
        scaled_grad = (grad_pre * row_scale).astype(jnp.bfloat16)
        grad_panels = lax.all_gather(scaled_grad, "rows", axis=0, tiled=True)
        back_part = aggregate_slots(grad_panels, tile_row, tile_col, tile_value, rep_count * block_count)
        back_total = lax.psum_scatter(back_part, "rep", scatter_dimension=0, tiled=True)
        back_sum = (back_total * row_scale).astype(jnp.bfloat16)
        partial_input = lax.dot_general(
            back_sum, weight[:, cols], (((1,), (1,)), ((), ())), preferred_element_type=jnp.float32
        )
        grad_input = partial_input if grad_input is None else grad_input + partial_input
        local_weight = lax.dot_general(
            features, back_sum, (((0,), (0,)), ((), ())), preferred_element_type=jnp.float32
        )
        weight_parts.append(all_reduce_by_exchange(local_weight, ("rows", "rep")))
    hidden_out = jnp.concatenate(hidden_parts, axis=1)
    grad_weight = jnp.concatenate(weight_parts, axis=1)
    return (hidden_out, grad_input.astype(jnp.bfloat16), grad_weight)


def solution(mesh):
    placed = (
        P(("rows", "rep"), None),
        P(),
        P(),
        P(("rows", "rep")),
        P(("rows", "rep")),
        P(("rows", "rep")),
        P(("rows", "rep"), None, None),
        P(("rows", "rep"), None),
    )
    return jax.shard_map(
        shards,
        mesh=mesh,
        in_specs=placed,
        out_specs=(P(("rows", "rep"), None), P(("rows", "rep"), None), P()),
        check_vma=False,
    )
```

```python
import jax
import jax.numpy as jnp
from jax import lax
from jax.experimental import pallas as pl
from jax.experimental.pallas import tpu as pltpu
from jax.sharding import PartitionSpec as P


PANEL_BUFFERS = 4


def _aggregate_kernel(rows_ref, cols_ref, tiles_ref, panels_hbm, out_ref, buffers, sems):
    slot_count, tile_size, _ = tiles_ref.shape
    panel_blocks = panels_hbm.shape[0] // tile_size
    out_blocks = out_ref.shape[0] // tile_size

    def panel_copy(s, buffer):
        col = jnp.clip(cols_ref[s], 0, panel_blocks - 1)
        start = pl.multiple_of(col * tile_size, tile_size)
        return pltpu.make_async_copy(
            panels_hbm.at[pl.ds(start, tile_size), :], buffers.at[buffer], sems.at[buffer]
        )

    for buffer in range(PANEL_BUFFERS):
        panel_copy(buffer, buffer).start()
    out_ref[...] = jnp.zeros_like(out_ref)

    def step(s, carry):
        buffer = s % PANEL_BUFFERS
        panel_copy(s, buffer).wait()
        row = jnp.clip(rows_ref[s], 0, out_blocks - 1)
        start = pl.multiple_of(row * tile_size, tile_size)
        product = jnp.dot(tiles_ref[s], buffers[buffer], preferred_element_type=jnp.float32)
        out_ref[pl.ds(start, tile_size), :] += product

        @pl.when(s + PANEL_BUFFERS < slot_count)
        def _():
            panel_copy(s + PANEL_BUFFERS, buffer).start()

        return carry

    lax.fori_loop(0, slot_count, step, 0)


def aggregate_slots(panels, group_rows, group_cols, tiles, out_blocks):
    slot_count, tile_size, _ = tiles.shape
    feat_width = panels.shape[1]
    grid_spec = pltpu.PrefetchScalarGridSpec(
        num_scalar_prefetch=2,
        grid=(1,),
        in_specs=[
            pl.BlockSpec((slot_count, tile_size, tile_size), lambda i, rows, cols: (0, 0, 0)),
            pl.BlockSpec(memory_space=pl.ANY),
        ],
        out_specs=pl.BlockSpec((out_blocks * tile_size, feat_width), lambda i, rows, cols: (0, 0)),
        scratch_shapes=[
            pltpu.VMEM((PANEL_BUFFERS, tile_size, feat_width), panels.dtype),
            pltpu.SemaphoreType.DMA((PANEL_BUFFERS,)),
        ],
    )
    return pl.pallas_call(
        _aggregate_kernel,
        grid_spec=grid_spec,
        out_shape=jax.ShapeDtypeStruct((out_blocks * tile_size, feat_width), jnp.float32),
        compiler_params=pltpu.CompilerParams(dimension_semantics=("arbitrary",)),
    )(group_rows, group_cols, tiles, panels)


def all_reduce_by_exchange(value, axes):
    count = 1
    for axis in axes:
        count *= lax.axis_size(axis)
    rows, width = value.shape
    chunks = lax.all_to_all(value.reshape(count, rows // count, width), axes, 0, 0, tiled=True)
    own = chunks.sum(axis=0)
    spread = jnp.broadcast_to(own[None], (count,) + own.shape)
    return lax.all_to_all(spread, axes, 0, 0, tiled=True).reshape(rows, width)


def shards(features, weight, out_bias, degree, tile_row, tile_col, tile_value, cotangent):
    tile_size = tile_value.shape[1]
    nodes_dev = features.shape[0]
    block_count = nodes_dev // tile_size
    rep_count = lax.axis_size("rep")
    row_scale = lax.rsqrt(degree.astype(jnp.float32))[:, None]
    scaled = (jnp.dot(features, weight, preferred_element_type=jnp.float32) * row_scale).astype(
        jnp.bfloat16
    )
    panels = lax.all_gather(scaled, "rows", axis=0, tiled=True)
    slab_part = aggregate_slots(panels, tile_row, tile_col, tile_value, rep_count * block_count)
    aggregate = lax.psum_scatter(slab_part, "rep", scatter_dimension=0, tiled=True) * row_scale
    pre_act = aggregate + out_bias
    hidden_out = jax.nn.silu(pre_act).astype(jnp.bfloat16)
    sigmoid_pre = jax.nn.sigmoid(pre_act)
    grad_pre = cotangent.astype(jnp.float32) * sigmoid_pre * (1.0 + pre_act * (1.0 - sigmoid_pre))
    scaled_grad = (grad_pre * row_scale).astype(jnp.bfloat16)
    grad_panels = lax.all_gather(scaled_grad, "rows", axis=0, tiled=True)
    back_part = aggregate_slots(grad_panels, tile_row, tile_col, tile_value, rep_count * block_count)
    back_total = lax.psum_scatter(back_part, "rep", scatter_dimension=0, tiled=True)
    back_sum = (back_total * row_scale).astype(jnp.bfloat16)
    grad_input = lax.dot_general(
        back_sum, weight, (((1,), (1,)), ((), ())), preferred_element_type=jnp.float32
    ).astype(jnp.bfloat16)
    local_weight = lax.dot_general(
        features, back_sum, (((0,), (0,)), ((), ())), preferred_element_type=jnp.float32
    )
    grad_weight = all_reduce_by_exchange(local_weight, ("rows", "rep"))
    return (hidden_out, grad_input, grad_weight)


def solution(mesh):
    placed = (
        P(("rows", "rep"), None),
        P(),
        P(),
        P(("rows", "rep")),
        P(("rows", "rep")),
        P(("rows", "rep")),
        P(("rows", "rep"), None, None),
        P(("rows", "rep"), None),
    )
    return jax.shard_map(
        shards,
        mesh=mesh,
        in_specs=placed,
        out_specs=(P(("rows", "rep"), None), P(("rows", "rep"), None), P()),
        check_vma=False,
    )
```

```python
import jax
import jax.numpy as jnp
from jax import lax
from jax.experimental import pallas as pl
from jax.experimental.pallas import tpu as pltpu
from jax.sharding import PartitionSpec as P


PANEL_BUFFERS = 4


def _aggregate_kernel(rows_ref, cols_ref, tiles_ref, panels_hbm, out_ref, buffers, sems):
    slot_count, tile_size, _ = tiles_ref.shape
    panel_blocks = panels_hbm.shape[0] // tile_size
    out_blocks = out_ref.shape[0] // tile_size

    def panel_copy(s, buffer):
        col = jnp.clip(cols_ref[s], 0, panel_blocks - 1)
        start = pl.multiple_of(col * tile_size, tile_size)
        return pltpu.make_async_copy(
            panels_hbm.at[pl.ds(start, tile_size), :], buffers.at[buffer], sems.at[buffer]
        )

    for buffer in range(PANEL_BUFFERS):
        panel_copy(buffer, buffer).start()
    out_ref[...] = jnp.zeros_like(out_ref)

    def step(s, carry):
        buffer = s % PANEL_BUFFERS
        panel_copy(s, buffer).wait()
        row = jnp.clip(rows_ref[s], 0, out_blocks - 1)
        start = pl.multiple_of(row * tile_size, tile_size)
        product = jnp.dot(tiles_ref[s], buffers[buffer], preferred_element_type=jnp.float32)
        out_ref[pl.ds(start, tile_size), :] += product

        @pl.when(s + PANEL_BUFFERS < slot_count)
        def _():
            panel_copy(s + PANEL_BUFFERS, buffer).start()

        return carry

    lax.fori_loop(0, slot_count, step, 0)


def aggregate_slots(panels, group_rows, group_cols, tiles, out_blocks):
    slot_count, tile_size, _ = tiles.shape
    feat_width = panels.shape[1]
    grid_spec = pltpu.PrefetchScalarGridSpec(
        num_scalar_prefetch=2,
        grid=(1,),
        in_specs=[
            pl.BlockSpec((slot_count, tile_size, tile_size), lambda i, rows, cols: (0, 0, 0)),
            pl.BlockSpec(memory_space=pl.ANY),
        ],
        out_specs=pl.BlockSpec((out_blocks * tile_size, feat_width), lambda i, rows, cols: (0, 0)),
        scratch_shapes=[
            pltpu.VMEM((PANEL_BUFFERS, tile_size, feat_width), panels.dtype),
            pltpu.SemaphoreType.DMA((PANEL_BUFFERS,)),
        ],
    )
    return pl.pallas_call(
        _aggregate_kernel,
        grid_spec=grid_spec,
        out_shape=jax.ShapeDtypeStruct((out_blocks * tile_size, feat_width), jnp.float32),
        compiler_params=pltpu.CompilerParams(dimension_semantics=("arbitrary",)),
    )(group_rows, group_cols, tiles, panels)


def all_reduce_by_exchange(value, axes):
    count = 1
    for axis in axes:
        count *= lax.axis_size(axis)
    rows, width = value.shape
    chunks = lax.all_to_all(value.reshape(count, rows // count, width), axes, 0, 0, tiled=True)
    own = chunks.sum(axis=0)
    spread = jnp.broadcast_to(own[None], (count,) + own.shape)
    return lax.all_to_all(spread, axes, 0, 0, tiled=True).reshape(rows, width)


def gather_by_exchange(value, axis):
    count = lax.axis_size(axis)
    copies = jnp.broadcast_to(value[None], (count,) + value.shape)
    return lax.all_to_all(copies, axis, 0, 0, tiled=True).reshape((-1,) + value.shape[1:])


def shards(features, weight, out_bias, degree, tile_row, tile_col, tile_value, cotangent):
    tile_size = tile_value.shape[1]
    nodes_dev = features.shape[0]
    block_count = nodes_dev // tile_size
    rep_count = lax.axis_size("rep")
    row_scale = lax.rsqrt(degree.astype(jnp.float32))[:, None]
    scaled = (jnp.dot(features, weight, preferred_element_type=jnp.float32) * row_scale).astype(
        jnp.bfloat16
    )
    panels = lax.all_gather(scaled, "rows", axis=0, tiled=True)
    slab_features = gather_by_exchange(features, "rep")
    slab_scale = gather_by_exchange(row_scale, "rep")
    slab_part = aggregate_slots(panels, tile_row, tile_col, tile_value, rep_count * block_count)
    aggregate = lax.psum_scatter(slab_part, "rep", scatter_dimension=0, tiled=True) * row_scale
    pre_act = aggregate + out_bias
    hidden_out = jax.nn.silu(pre_act).astype(jnp.bfloat16)
    sigmoid_pre = jax.nn.sigmoid(pre_act)
    grad_pre = cotangent.astype(jnp.float32) * sigmoid_pre * (1.0 + pre_act * (1.0 - sigmoid_pre))
    scaled_grad = (grad_pre * row_scale).astype(jnp.bfloat16)
    grad_panels = lax.all_gather(scaled_grad, "rows", axis=0, tiled=True)
    back_part = aggregate_slots(grad_panels, tile_row, tile_col, tile_value, rep_count * block_count)
    back_total = lax.psum_scatter(back_part, "rep", scatter_dimension=0, tiled=True)
    back_sum = (back_total * row_scale).astype(jnp.bfloat16)
    grad_input = lax.dot_general(
        back_sum, weight, (((1,), (1,)), ((), ())), preferred_element_type=jnp.float32
    ).astype(jnp.bfloat16)
    local_weight = lax.dot_general(
        slab_features, back_part * slab_scale, (((0,), (0,)), ((), ())), preferred_element_type=jnp.float32
    )
    grad_weight = all_reduce_by_exchange(local_weight, ("rows", "rep"))
    return (hidden_out, grad_input, grad_weight)


def solution(mesh):
    placed = (
        P(("rows", "rep"), None),
        P(),
        P(),
        P(("rows", "rep")),
        P(("rows", "rep")),
        P(("rows", "rep")),
        P(("rows", "rep"), None, None),
        P(("rows", "rep"), None),
    )
    return jax.shard_map(
        shards,
        mesh=mesh,
        in_specs=placed,
        out_specs=(P(("rows", "rep"), None), P(("rows", "rep"), None), P()),
        check_vma=False,
    )
```

```python
import jax
import jax.numpy as jnp
from jax import lax
from jax.experimental import pallas as pl
from jax.experimental.pallas import tpu as pltpu
from jax.sharding import PartitionSpec as P


PANEL_BUFFERS = 4


def _aggregate_kernel(rows_ref, cols_ref, tiles_ref, panels_hbm, out_ref, buffers, sems):
    slot_count, tile_size, _ = tiles_ref.shape
    panel_blocks = panels_hbm.shape[0] // tile_size
    out_blocks = out_ref.shape[0] // tile_size

    def panel_copy(s, buffer):
        col = jnp.clip(cols_ref[s], 0, panel_blocks - 1)
        start = pl.multiple_of(col * tile_size, tile_size)
        return pltpu.make_async_copy(
            panels_hbm.at[pl.ds(start, tile_size), :], buffers.at[buffer], sems.at[buffer]
        )

    for buffer in range(PANEL_BUFFERS):
        panel_copy(buffer, buffer).start()
    out_ref[...] = jnp.zeros_like(out_ref)

    def step(s, carry):
        buffer = s % PANEL_BUFFERS
        panel_copy(s, buffer).wait()
        row = jnp.clip(rows_ref[s], 0, out_blocks - 1)
        start = pl.multiple_of(row * tile_size, tile_size)
        product = jnp.dot(tiles_ref[s], buffers[buffer], preferred_element_type=jnp.float32)
        out_ref[pl.ds(start, tile_size), :] += product

        @pl.when(s + PANEL_BUFFERS < slot_count)
        def _():
            panel_copy(s + PANEL_BUFFERS, buffer).start()

        return carry

    lax.fori_loop(0, slot_count, step, 0)


def aggregate_slots(panels, group_rows, group_cols, tiles, out_blocks):
    slot_count, tile_size, _ = tiles.shape
    feat_width = panels.shape[1]
    grid_spec = pltpu.PrefetchScalarGridSpec(
        num_scalar_prefetch=2,
        grid=(1,),
        in_specs=[
            pl.BlockSpec((slot_count, tile_size, tile_size), lambda i, rows, cols: (0, 0, 0)),
            pl.BlockSpec(memory_space=pl.ANY),
        ],
        out_specs=pl.BlockSpec((out_blocks * tile_size, feat_width), lambda i, rows, cols: (0, 0)),
        scratch_shapes=[
            pltpu.VMEM((PANEL_BUFFERS, tile_size, feat_width), panels.dtype),
            pltpu.SemaphoreType.DMA((PANEL_BUFFERS,)),
        ],
    )
    return pl.pallas_call(
        _aggregate_kernel,
        grid_spec=grid_spec,
        out_shape=jax.ShapeDtypeStruct((out_blocks * tile_size, feat_width), jnp.float32),
        compiler_params=pltpu.CompilerParams(dimension_semantics=("arbitrary",)),
    )(group_rows, group_cols, tiles, panels)


def all_reduce_by_exchange(value, axes):
    count = 1
    for axis in axes:
        count *= lax.axis_size(axis)
    rows, width = value.shape
    chunks = lax.all_to_all(value.reshape(count, rows // count, width), axes, 0, 0, tiled=True)
    own = chunks.sum(axis=0)
    spread = jnp.broadcast_to(own[None], (count,) + own.shape)
    return lax.all_to_all(spread, axes, 0, 0, tiled=True).reshape(rows, width)


def gather_by_exchange(value, axis):
    count = lax.axis_size(axis)
    copies = jnp.broadcast_to(value[None], (count,) + value.shape)
    return lax.all_to_all(copies, axis, 0, 0, tiled=True).reshape((-1,) + value.shape[1:])


def shards(features, weight, out_bias, degree, tile_row, tile_col, tile_value, cotangent):
    tile_size = tile_value.shape[1]
    nodes_dev = features.shape[0]
    block_count = nodes_dev // tile_size
    rep_count = lax.axis_size("rep")
    row_scale = lax.rsqrt(degree.astype(jnp.float32))[:, None]
    scaled = (jnp.dot(features, weight, preferred_element_type=jnp.float32) * row_scale).astype(
        jnp.bfloat16
    )
    panels = lax.all_gather(scaled, "rows", axis=0, tiled=True)
    slab_features = gather_by_exchange(features, "rep")
    slab_scale = gather_by_exchange(row_scale, "rep")
    panels, slab_features, slab_scale = lax.optimization_barrier((panels, slab_features, slab_scale))
    slab_part = aggregate_slots(panels, tile_row, tile_col, tile_value, rep_count * block_count)
    aggregate = lax.psum_scatter(slab_part, "rep", scatter_dimension=0, tiled=True) * row_scale
    pre_act = aggregate + out_bias
    hidden_out = jax.nn.silu(pre_act).astype(jnp.bfloat16)
    sigmoid_pre = jax.nn.sigmoid(pre_act)
    grad_pre = cotangent.astype(jnp.float32) * sigmoid_pre * (1.0 + pre_act * (1.0 - sigmoid_pre))
    scaled_grad = (grad_pre * row_scale).astype(jnp.bfloat16)
    grad_panels = lax.all_gather(scaled_grad, "rows", axis=0, tiled=True)
    back_part = aggregate_slots(grad_panels, tile_row, tile_col, tile_value, rep_count * block_count)
    back_total = lax.psum_scatter(back_part, "rep", scatter_dimension=0, tiled=True)
    back_sum = (back_total * row_scale).astype(jnp.bfloat16)
    grad_input = lax.dot_general(
        back_sum, weight, (((1,), (1,)), ((), ())), preferred_element_type=jnp.float32
    ).astype(jnp.bfloat16)
    local_weight = lax.dot_general(
        slab_features, back_part * slab_scale, (((0,), (0,)), ((), ())), preferred_element_type=jnp.float32
    )
    grad_weight = all_reduce_by_exchange(local_weight, ("rows", "rep"))
    return (hidden_out, grad_input, grad_weight)


def solution(mesh):
    placed = (
        P(("rows", "rep"), None),
        P(),
        P(),
        P(("rows", "rep")),
        P(("rows", "rep")),
        P(("rows", "rep")),
        P(("rows", "rep"), None, None),
        P(("rows", "rep"), None),
    )
    return jax.shard_map(
        shards,
        mesh=mesh,
        in_specs=placed,
        out_specs=(P(("rows", "rep"), None), P(("rows", "rep"), None), P()),
        check_vma=False,
    )
```

```python
import jax
import jax.numpy as jnp
from jax import lax
from jax.experimental import pallas as pl
from jax.experimental.pallas import tpu as pltpu
from jax.sharding import PartitionSpec as P


PANEL_BUFFERS = 8


def _aggregate_kernel(rows_ref, cols_ref, tiles_ref, panels_hbm, out_ref, buffers, sems):
    slot_count, tile_size, _ = tiles_ref.shape
    panel_blocks = panels_hbm.shape[0] // tile_size
    out_blocks = out_ref.shape[0] // tile_size

    def panel_copy(s, buffer):
        col = jnp.clip(cols_ref[s], 0, panel_blocks - 1)
        start = pl.multiple_of(col * tile_size, tile_size)
        return pltpu.make_async_copy(
            panels_hbm.at[pl.ds(start, tile_size), :], buffers.at[buffer], sems.at[buffer]
        )

    for buffer in range(PANEL_BUFFERS):
        panel_copy(buffer, buffer).start()
    out_ref[...] = jnp.zeros_like(out_ref)

    def step(s, carry):
        buffer = s % PANEL_BUFFERS
        panel_copy(s, buffer).wait()
        row = jnp.clip(rows_ref[s], 0, out_blocks - 1)
        start = pl.multiple_of(row * tile_size, tile_size)
        product = jnp.dot(tiles_ref[s], buffers[buffer], preferred_element_type=jnp.float32)
        out_ref[pl.ds(start, tile_size), :] += product

        @pl.when(s + PANEL_BUFFERS < slot_count)
        def _():
            panel_copy(s + PANEL_BUFFERS, buffer).start()

        return carry

    lax.fori_loop(0, slot_count, step, 0, unroll=2)


def aggregate_slots(panels, group_rows, group_cols, tiles, out_blocks):
    slot_count, tile_size, _ = tiles.shape
    feat_width = panels.shape[1]
    grid_spec = pltpu.PrefetchScalarGridSpec(
        num_scalar_prefetch=2,
        grid=(1,),
        in_specs=[
            pl.BlockSpec((slot_count, tile_size, tile_size), lambda i, rows, cols: (0, 0, 0)),
            pl.BlockSpec(memory_space=pl.ANY),
        ],
        out_specs=pl.BlockSpec((out_blocks * tile_size, feat_width), lambda i, rows, cols: (0, 0)),
        scratch_shapes=[
            pltpu.VMEM((PANEL_BUFFERS, tile_size, feat_width), panels.dtype),
            pltpu.SemaphoreType.DMA((PANEL_BUFFERS,)),
        ],
    )
    return pl.pallas_call(
        _aggregate_kernel,
        grid_spec=grid_spec,
        out_shape=jax.ShapeDtypeStruct((out_blocks * tile_size, feat_width), jnp.float32),
        compiler_params=pltpu.CompilerParams(dimension_semantics=("arbitrary",)),
    )(group_rows, group_cols, tiles, panels)


def all_reduce_by_exchange(value, axes):
    count = 1
    for axis in axes:
        count *= lax.axis_size(axis)
    rows, width = value.shape
    chunks = lax.all_to_all(value.reshape(count, rows // count, width), axes, 0, 0, tiled=True)
    own = chunks.sum(axis=0)
    spread = jnp.broadcast_to(own[None], (count,) + own.shape)
    return lax.all_to_all(spread, axes, 0, 0, tiled=True).reshape(rows, width)


def gather_by_exchange(value, axis):
    count = lax.axis_size(axis)
    copies = jnp.broadcast_to(value[None], (count,) + value.shape)
    return lax.all_to_all(copies, axis, 0, 0, tiled=True).reshape((-1,) + value.shape[1:])


def shards(features, weight, out_bias, degree, tile_row, tile_col, tile_value, cotangent):
    tile_size = tile_value.shape[1]
    nodes_dev = features.shape[0]
    block_count = nodes_dev // tile_size
    rep_count = lax.axis_size("rep")
    row_scale = lax.rsqrt(degree.astype(jnp.float32))[:, None]
    scaled = (jnp.dot(features, weight, preferred_element_type=jnp.float32) * row_scale).astype(
        jnp.bfloat16
    )
    panels = lax.all_gather(scaled, "rows", axis=0, tiled=True)
    slab_features = gather_by_exchange(features, "rep")
    slab_scale = gather_by_exchange(row_scale, "rep")
    panels, slab_features, slab_scale = lax.optimization_barrier((panels, slab_features, slab_scale))
    slab_part = aggregate_slots(panels, tile_row, tile_col, tile_value, rep_count * block_count)
    aggregate = lax.psum_scatter(slab_part, "rep", scatter_dimension=0, tiled=True) * row_scale
    pre_act = aggregate + out_bias
    hidden_out = jax.nn.silu(pre_act).astype(jnp.bfloat16)
    sigmoid_pre = jax.nn.sigmoid(pre_act)
    grad_pre = cotangent.astype(jnp.float32) * sigmoid_pre * (1.0 + pre_act * (1.0 - sigmoid_pre))
    scaled_grad = (grad_pre * row_scale).astype(jnp.bfloat16)
    grad_panels = lax.all_gather(scaled_grad, "rows", axis=0, tiled=True)
    back_part = aggregate_slots(grad_panels, tile_row, tile_col, tile_value, rep_count * block_count)
    back_total = lax.psum_scatter(back_part, "rep", scatter_dimension=0, tiled=True)
    back_sum = (back_total * row_scale).astype(jnp.bfloat16)
    grad_input = lax.dot_general(
        back_sum, weight, (((1,), (1,)), ((), ())), preferred_element_type=jnp.float32
    ).astype(jnp.bfloat16)
    local_weight = lax.dot_general(
        slab_features, back_part * slab_scale, (((0,), (0,)), ((), ())), preferred_element_type=jnp.float32
    )
    grad_weight = all_reduce_by_exchange(local_weight, ("rows", "rep"))
    return (hidden_out, grad_input, grad_weight)


def solution(mesh):
    placed = (
        P(("rows", "rep"), None),
        P(),
        P(),
        P(("rows", "rep")),
        P(("rows", "rep")),
        P(("rows", "rep")),
        P(("rows", "rep"), None, None),
        P(("rows", "rep"), None),
    )
    return jax.shard_map(
        shards,
        mesh=mesh,
        in_specs=placed,
        out_specs=(P(("rows", "rep"), None), P(("rows", "rep"), None), P()),
        check_vma=False,
    )
```

```python
import jax
import jax.numpy as jnp
from jax import lax
from jax.experimental import pallas as pl
from jax.experimental.pallas import tpu as pltpu
from jax.sharding import PartitionSpec as P


PANEL_BUFFERS = 8


def _aggregate_kernel(rows_ref, cols_ref, tiles_ref, panels_hbm, out_ref, buffers, sems):
    slot_count, tile_size, _ = tiles_ref.shape
    panel_blocks = panels_hbm.shape[0] // tile_size
    out_blocks = out_ref.shape[0] // tile_size

    def panel_copy(s, buffer):
        col = jnp.clip(cols_ref[s], 0, panel_blocks - 1)
        start = pl.multiple_of(col * tile_size, tile_size)
        return pltpu.make_async_copy(
            panels_hbm.at[pl.ds(start, tile_size), :], buffers.at[buffer], sems.at[buffer]
        )

    for buffer in range(PANEL_BUFFERS):
        panel_copy(buffer, buffer).start()
    out_ref[...] = jnp.zeros_like(out_ref)

    def step(s, carry):
        buffer = s % PANEL_BUFFERS
        panel_copy(s, buffer).wait()
        row = jnp.clip(rows_ref[s], 0, out_blocks - 1)
        start = pl.multiple_of(row * tile_size, tile_size)
        product = jnp.dot(tiles_ref[s], buffers[buffer], preferred_element_type=jnp.float32)
        out_ref[pl.ds(start, tile_size), :] += product

        @pl.when(s + PANEL_BUFFERS < slot_count)
        def _():
            panel_copy(s + PANEL_BUFFERS, buffer).start()

        return carry

    lax.fori_loop(0, slot_count, step, 0, unroll=2)


def aggregate_slots(panels, group_rows, group_cols, tiles, out_blocks):
    slot_count, tile_size, _ = tiles.shape
    feat_width = panels.shape[1]
    grid_spec = pltpu.PrefetchScalarGridSpec(
        num_scalar_prefetch=2,
        grid=(1,),
        in_specs=[
            pl.BlockSpec((slot_count, tile_size, tile_size), lambda i, rows, cols: (0, 0, 0)),
            pl.BlockSpec(memory_space=pl.ANY),
        ],
        out_specs=pl.BlockSpec((out_blocks * tile_size, feat_width), lambda i, rows, cols: (0, 0)),
        scratch_shapes=[
            pltpu.VMEM((PANEL_BUFFERS, tile_size, feat_width), panels.dtype),
            pltpu.SemaphoreType.DMA((PANEL_BUFFERS,)),
        ],
    )
    return pl.pallas_call(
        _aggregate_kernel,
        grid_spec=grid_spec,
        out_shape=jax.ShapeDtypeStruct((out_blocks * tile_size, feat_width), jnp.float32),
        compiler_params=pltpu.CompilerParams(dimension_semantics=("arbitrary",)),
    )(group_rows, group_cols, tiles, panels)


def all_reduce_by_exchange(value, axes):
    count = 1
    for axis in axes:
        count *= lax.axis_size(axis)
    rows, width = value.shape
    chunks = lax.all_to_all(value.reshape(count, rows // count, width), axes, 0, 0, tiled=True)
    own = chunks.sum(axis=0)
    spread = jnp.broadcast_to(own[None], (count,) + own.shape)
    return lax.all_to_all(spread, axes, 0, 0, tiled=True).reshape(rows, width)


def gather_by_exchange(value, axis):
    count = lax.axis_size(axis)
    copies = jnp.broadcast_to(value[None], (count,) + value.shape)
    return lax.all_to_all(copies, axis, 0, 0, tiled=True).reshape((-1,) + value.shape[1:])


def shards(features, weight, out_bias, degree, tile_row, tile_col, tile_value, cotangent):
    tile_size = tile_value.shape[1]
    nodes_dev = features.shape[0]
    block_count = nodes_dev // tile_size
    rep_count = lax.axis_size("rep")
    row_scale = lax.rsqrt(degree.astype(jnp.float32))[:, None]
    scaled = (jnp.dot(features, weight, preferred_element_type=jnp.float32) * row_scale).astype(
        jnp.bfloat16
    )
    panels = lax.all_gather(scaled, "rows", axis=0, tiled=True)
    slab_features = gather_by_exchange(features, "rep")
    slab_scale = gather_by_exchange(row_scale, "rep")
    panels, slab_features, slab_scale = lax.optimization_barrier((panels, slab_features, slab_scale))
    slab_part = aggregate_slots(panels, tile_row, tile_col, tile_value, rep_count * block_count)
    aggregate = lax.psum_scatter(slab_part, "rep", scatter_dimension=0, tiled=True) * row_scale
    pre_act = aggregate + out_bias
    hidden_out = jax.nn.silu(pre_act).astype(jnp.bfloat16)
    sigmoid_pre = jax.nn.sigmoid(pre_act)
    grad_pre = cotangent.astype(jnp.float32) * sigmoid_pre * (1.0 + pre_act * (1.0 - sigmoid_pre))
    scaled_grad = (grad_pre * row_scale).astype(jnp.bfloat16)
    grad_panels = lax.all_gather(scaled_grad, "rows", axis=0, tiled=True)
    back_part = aggregate_slots(grad_panels, tile_row, tile_col, tile_value, rep_count * block_count)
    back_total = lax.psum_scatter(back_part.astype(jnp.bfloat16), "rep", scatter_dimension=0, tiled=True)
    back_sum = (back_total.astype(jnp.float32) * row_scale).astype(jnp.bfloat16)
    grad_input = lax.dot_general(
        back_sum, weight, (((1,), (1,)), ((), ())), preferred_element_type=jnp.float32
    ).astype(jnp.bfloat16)
    local_weight = lax.dot_general(
        slab_features, back_part * slab_scale, (((0,), (0,)), ((), ())), preferred_element_type=jnp.float32
    )
    grad_weight = all_reduce_by_exchange(local_weight, ("rows", "rep"))
    return (hidden_out, grad_input, grad_weight)


def solution(mesh):
    placed = (
        P(("rows", "rep"), None),
        P(),
        P(),
        P(("rows", "rep")),
        P(("rows", "rep")),
        P(("rows", "rep")),
        P(("rows", "rep"), None, None),
        P(("rows", "rep"), None),
    )
    return jax.shard_map(
        shards,
        mesh=mesh,
        in_specs=placed,
        out_specs=(P(("rows", "rep"), None), P(("rows", "rep"), None), P()),
        check_vma=False,
    )
```

```python
import jax
import jax.numpy as jnp
from jax import lax
from jax.experimental import pallas as pl
from jax.experimental.pallas import tpu as pltpu
from jax.sharding import PartitionSpec as P


PANEL_BUFFERS = 16


def _aggregate_kernel(rows_ref, cols_ref, tiles_ref, panels_hbm, out_ref, buffers, sems):
    slot_count, tile_size, _ = tiles_ref.shape
    panel_blocks = panels_hbm.shape[0] // tile_size
    out_blocks = out_ref.shape[0] // tile_size

    def panel_copy(s, buffer):
        col = jnp.clip(cols_ref[s], 0, panel_blocks - 1)
        start = pl.multiple_of(col * tile_size, tile_size)
        return pltpu.make_async_copy(
            panels_hbm.at[pl.ds(start, tile_size), :], buffers.at[buffer], sems.at[buffer]
        )

    for buffer in range(PANEL_BUFFERS):
        panel_copy(buffer, buffer).start()
    out_ref[...] = jnp.zeros_like(out_ref)

    def step(s, carry):
        buffer = s % PANEL_BUFFERS
        panel_copy(s, buffer).wait()
        row = jnp.clip(rows_ref[s], 0, out_blocks - 1)
        start = pl.multiple_of(row * tile_size, tile_size)
        product = jnp.dot(tiles_ref[s], buffers[buffer], preferred_element_type=jnp.float32)
        out_ref[pl.ds(start, tile_size), :] += product

        @pl.when(s + PANEL_BUFFERS < slot_count)
        def _():
            panel_copy(s + PANEL_BUFFERS, buffer).start()

        return carry

    lax.fori_loop(0, slot_count, step, 0, unroll=4)


def aggregate_slots(panels, group_rows, group_cols, tiles, out_blocks):
    slot_count, tile_size, _ = tiles.shape
    feat_width = panels.shape[1]
    grid_spec = pltpu.PrefetchScalarGridSpec(
        num_scalar_prefetch=2,
        grid=(1,),
        in_specs=[
            pl.BlockSpec((slot_count, tile_size, tile_size), lambda i, rows, cols: (0, 0, 0)),
            pl.BlockSpec(memory_space=pl.ANY),
        ],
        out_specs=pl.BlockSpec((out_blocks * tile_size, feat_width), lambda i, rows, cols: (0, 0)),
        scratch_shapes=[
            pltpu.VMEM((PANEL_BUFFERS, tile_size, feat_width), panels.dtype),
            pltpu.SemaphoreType.DMA((PANEL_BUFFERS,)),
        ],
    )
    return pl.pallas_call(
        _aggregate_kernel,
        grid_spec=grid_spec,
        out_shape=jax.ShapeDtypeStruct((out_blocks * tile_size, feat_width), jnp.float32),
        compiler_params=pltpu.CompilerParams(dimension_semantics=("arbitrary",)),
    )(group_rows, group_cols, tiles, panels)


def all_reduce_by_exchange(value, axes):
    count = 1
    for axis in axes:
        count *= lax.axis_size(axis)
    rows, width = value.shape
    chunks = lax.all_to_all(value.reshape(count, rows // count, width), axes, 0, 0, tiled=True)
    own = chunks.sum(axis=0)
    spread = jnp.broadcast_to(own[None], (count,) + own.shape)
    return lax.all_to_all(spread, axes, 0, 0, tiled=True).reshape(rows, width)


def gather_by_exchange(value, axis):
    count = lax.axis_size(axis)
    copies = jnp.broadcast_to(value[None], (count,) + value.shape)
    return lax.all_to_all(copies, axis, 0, 0, tiled=True).reshape((-1,) + value.shape[1:])


def shards(features, weight, out_bias, degree, tile_row, tile_col, tile_value, cotangent):
    tile_size = tile_value.shape[1]
    nodes_dev = features.shape[0]
    block_count = nodes_dev // tile_size
    rep_count = lax.axis_size("rep")
    row_scale = lax.rsqrt(degree.astype(jnp.float32))[:, None]
    scaled = (jnp.dot(features, weight, preferred_element_type=jnp.float32) * row_scale).astype(
        jnp.bfloat16
    )
    panels = lax.all_gather(scaled, "rows", axis=0, tiled=True)
    slab_features = gather_by_exchange(features, "rep")
    slab_scale = gather_by_exchange(row_scale, "rep")
    panels, slab_features, slab_scale = lax.optimization_barrier((panels, slab_features, slab_scale))
    slab_part = aggregate_slots(panels, tile_row, tile_col, tile_value, rep_count * block_count)
    aggregate = lax.psum_scatter(slab_part, "rep", scatter_dimension=0, tiled=True) * row_scale
    pre_act = aggregate + out_bias
    hidden_out = jax.nn.silu(pre_act).astype(jnp.bfloat16)
    sigmoid_pre = jax.nn.sigmoid(pre_act)
    grad_pre = cotangent.astype(jnp.float32) * sigmoid_pre * (1.0 + pre_act * (1.0 - sigmoid_pre))
    scaled_grad = (grad_pre * row_scale).astype(jnp.bfloat16)
    grad_panels = lax.all_gather(scaled_grad, "rows", axis=0, tiled=True)
    back_part = aggregate_slots(grad_panels, tile_row, tile_col, tile_value, rep_count * block_count)
    back_total = lax.psum_scatter(back_part, "rep", scatter_dimension=0, tiled=True)
    back_sum = (back_total * row_scale).astype(jnp.bfloat16)
    grad_input = lax.dot_general(
        back_sum, weight, (((1,), (1,)), ((), ())), preferred_element_type=jnp.float32
    ).astype(jnp.bfloat16)
    local_weight = lax.dot_general(
        slab_features, back_part * slab_scale, (((0,), (0,)), ((), ())), preferred_element_type=jnp.float32
    )
    grad_weight = all_reduce_by_exchange(local_weight, ("rows", "rep"))
    return (hidden_out, grad_input, grad_weight)


def solution(mesh):
    placed = (
        P(("rows", "rep"), None),
        P(),
        P(),
        P(("rows", "rep")),
        P(("rows", "rep")),
        P(("rows", "rep")),
        P(("rows", "rep"), None, None),
        P(("rows", "rep"), None),
    )
    return jax.shard_map(
        shards,
        mesh=mesh,
        in_specs=placed,
        out_specs=(P(("rows", "rep"), None), P(("rows", "rep"), None), P()),
        check_vma=False,
    )
```

```python
import jax
import jax.numpy as jnp
from jax import lax
from jax.experimental import pallas as pl
from jax.experimental.pallas import tpu as pltpu
from jax.sharding import PartitionSpec as P


PANEL_BUFFERS = 8


def _aggregate_kernel(rows_ref, cols_ref, tiles_hbm, panels_hbm, out_ref, buffers, tile_buffers, sems, tile_sems):
    slot_count, tile_size, _ = tiles_hbm.shape
    panel_blocks = panels_hbm.shape[0] // tile_size
    out_blocks = out_ref.shape[0] // tile_size

    def panel_copy(s, buffer):
        col = jnp.clip(cols_ref[s], 0, panel_blocks - 1)
        start = pl.multiple_of(col * tile_size, tile_size)
        return pltpu.make_async_copy(
            panels_hbm.at[pl.ds(start, tile_size), :], buffers.at[buffer], sems.at[buffer]
        )

    def tile_copy(s, buffer):
        return pltpu.make_async_copy(tiles_hbm.at[s], tile_buffers.at[buffer], tile_sems.at[buffer])

    for buffer in range(PANEL_BUFFERS):
        tile_copy(buffer, buffer).start()
        panel_copy(buffer, buffer).start()
    out_ref[...] = jnp.zeros_like(out_ref)

    def step(s, carry):
        buffer = s % PANEL_BUFFERS
        tile_copy(s, buffer).wait()
        panel_copy(s, buffer).wait()
        row = jnp.clip(rows_ref[s], 0, out_blocks - 1)
        start = pl.multiple_of(row * tile_size, tile_size)
        product = jnp.dot(tile_buffers[buffer], buffers[buffer], preferred_element_type=jnp.float32)
        out_ref[pl.ds(start, tile_size), :] += product

        @pl.when(s + PANEL_BUFFERS < slot_count)
        def _():
            tile_copy(s + PANEL_BUFFERS, buffer).start()
            panel_copy(s + PANEL_BUFFERS, buffer).start()

        return carry

    lax.fori_loop(0, slot_count, step, 0, unroll=2)


def aggregate_slots(panels, group_rows, group_cols, tiles, out_blocks):
    slot_count, tile_size, _ = tiles.shape
    feat_width = panels.shape[1]
    grid_spec = pltpu.PrefetchScalarGridSpec(
        num_scalar_prefetch=2,
        grid=(1,),
        in_specs=[
            pl.BlockSpec(memory_space=pl.ANY),
            pl.BlockSpec(memory_space=pl.ANY),
        ],
        out_specs=pl.BlockSpec((out_blocks * tile_size, feat_width), lambda i, rows, cols: (0, 0)),
        scratch_shapes=[
            pltpu.VMEM((PANEL_BUFFERS, tile_size, feat_width), panels.dtype),
            pltpu.VMEM((PANEL_BUFFERS, tile_size, tile_size), tiles.dtype),
            pltpu.SemaphoreType.DMA((PANEL_BUFFERS,)),
            pltpu.SemaphoreType.DMA((PANEL_BUFFERS,)),
        ],
    )
    return pl.pallas_call(
        _aggregate_kernel,
        grid_spec=grid_spec,
        out_shape=jax.ShapeDtypeStruct((out_blocks * tile_size, feat_width), jnp.float32),
        compiler_params=pltpu.CompilerParams(dimension_semantics=("arbitrary",)),
    )(group_rows, group_cols, tiles, panels)


def all_reduce_by_exchange(value, axes):
    count = 1
    for axis in axes:
        count *= lax.axis_size(axis)
    rows, width = value.shape
    chunks = lax.all_to_all(value.reshape(count, rows // count, width), axes, 0, 0, tiled=True)
    own = chunks.sum(axis=0)
    spread = jnp.broadcast_to(own[None], (count,) + own.shape)
    return lax.all_to_all(spread, axes, 0, 0, tiled=True).reshape(rows, width)


def gather_by_exchange(value, axis):
    count = lax.axis_size(axis)
    copies = jnp.broadcast_to(value[None], (count,) + value.shape)
    return lax.all_to_all(copies, axis, 0, 0, tiled=True).reshape((-1,) + value.shape[1:])


def shards(features, weight, out_bias, degree, tile_row, tile_col, tile_value, cotangent):
    tile_size = tile_value.shape[1]
    nodes_dev = features.shape[0]
    block_count = nodes_dev // tile_size
    rep_count = lax.axis_size("rep")
    row_scale = lax.rsqrt(degree.astype(jnp.float32))[:, None]
    scaled = (jnp.dot(features, weight, preferred_element_type=jnp.float32) * row_scale).astype(
        jnp.bfloat16
    )
    panels = lax.all_gather(scaled, "rows", axis=0, tiled=True)
    slab_features = gather_by_exchange(features, "rep")
    slab_scale = gather_by_exchange(row_scale, "rep")
    panels, slab_features, slab_scale = lax.optimization_barrier((panels, slab_features, slab_scale))
    slab_part = aggregate_slots(panels, tile_row, tile_col, tile_value, rep_count * block_count)
    aggregate = lax.psum_scatter(slab_part, "rep", scatter_dimension=0, tiled=True) * row_scale
    pre_act = aggregate + out_bias
    hidden_out = jax.nn.silu(pre_act).astype(jnp.bfloat16)
    sigmoid_pre = jax.nn.sigmoid(pre_act)
    grad_pre = cotangent.astype(jnp.float32) * sigmoid_pre * (1.0 + pre_act * (1.0 - sigmoid_pre))
    scaled_grad = (grad_pre * row_scale).astype(jnp.bfloat16)
    grad_panels = lax.all_gather(scaled_grad, "rows", axis=0, tiled=True)
    back_part = aggregate_slots(grad_panels, tile_row, tile_col, tile_value, rep_count * block_count)
    back_total = lax.psum_scatter(back_part, "rep", scatter_dimension=0, tiled=True)
    back_sum = (back_total * row_scale).astype(jnp.bfloat16)
    grad_input = lax.dot_general(
        back_sum, weight, (((1,), (1,)), ((), ())), preferred_element_type=jnp.float32
    ).astype(jnp.bfloat16)
    local_weight = lax.dot_general(
        slab_features, back_part * slab_scale, (((0,), (0,)), ((), ())), preferred_element_type=jnp.float32
    )
    grad_weight = all_reduce_by_exchange(local_weight, ("rows", "rep"))
    return (hidden_out, grad_input, grad_weight)


def solution(mesh):
    placed = (
        P(("rows", "rep"), None),
        P(),
        P(),
        P(("rows", "rep")),
        P(("rows", "rep")),
        P(("rows", "rep")),
        P(("rows", "rep"), None, None),
        P(("rows", "rep"), None),
    )
    return jax.shard_map(
        shards,
        mesh=mesh,
        in_specs=placed,
        out_specs=(P(("rows", "rep"), None), P(("rows", "rep"), None), P()),
        check_vma=False,
    )
```

```python
import jax
import jax.numpy as jnp
from jax import lax
from jax.experimental import pallas as pl
from jax.experimental.pallas import tpu as pltpu
from jax.sharding import PartitionSpec as P


PANEL_BUFFERS = 8


def _aggregate_kernel(rows_ref, cols_ref, tiles_hbm, panels_hbm, out_ref, buffers, tile_buffers, sems, tile_sems):
    slot_count, tile_size, _ = tiles_hbm.shape
    panel_blocks = panels_hbm.shape[0] // tile_size
    out_blocks = out_ref.shape[0] // tile_size

    def panel_copy(s, buffer):
        col = jnp.clip(cols_ref[s], 0, panel_blocks - 1)
        start = pl.multiple_of(col * tile_size, tile_size)
        return pltpu.make_async_copy(
            panels_hbm.at[pl.ds(start, tile_size), :], buffers.at[buffer], sems.at[buffer]
        )

    def tile_copy(s, buffer):
        return pltpu.make_async_copy(tiles_hbm.at[s], tile_buffers.at[buffer], tile_sems.at[buffer])

    for buffer in range(PANEL_BUFFERS):
        tile_copy(buffer, buffer).start()
        panel_copy(buffer, buffer).start()
    out_ref[...] = jnp.zeros_like(out_ref)

    def step(s, carry):
        buffer = s % PANEL_BUFFERS
        tile_copy(s, buffer).wait()
        panel_copy(s, buffer).wait()
        row = jnp.clip(rows_ref[s], 0, out_blocks - 1)
        start = pl.multiple_of(row * tile_size, tile_size)
        product = jnp.dot(tile_buffers[buffer], buffers[buffer], preferred_element_type=jnp.float32)
        out_ref[pl.ds(start, tile_size), :] += product

        @pl.when(s + PANEL_BUFFERS < slot_count)
        def _():
            tile_copy(s + PANEL_BUFFERS, buffer).start()
            panel_copy(s + PANEL_BUFFERS, buffer).start()

        return carry

    lax.fori_loop(0, slot_count, step, 0, unroll=8)


def aggregate_slots(panels, group_rows, group_cols, tiles, out_blocks):
    slot_count, tile_size, _ = tiles.shape
    feat_width = panels.shape[1]
    grid_spec = pltpu.PrefetchScalarGridSpec(
        num_scalar_prefetch=2,
        grid=(1,),
        in_specs=[
            pl.BlockSpec(memory_space=pl.ANY),
            pl.BlockSpec(memory_space=pl.ANY),
        ],
        out_specs=pl.BlockSpec((out_blocks * tile_size, feat_width), lambda i, rows, cols: (0, 0)),
        scratch_shapes=[
            pltpu.VMEM((PANEL_BUFFERS, tile_size, feat_width), panels.dtype),
            pltpu.VMEM((PANEL_BUFFERS, tile_size, tile_size), tiles.dtype),
            pltpu.SemaphoreType.DMA((PANEL_BUFFERS,)),
            pltpu.SemaphoreType.DMA((PANEL_BUFFERS,)),
        ],
    )
    return pl.pallas_call(
        _aggregate_kernel,
        grid_spec=grid_spec,
        out_shape=jax.ShapeDtypeStruct((out_blocks * tile_size, feat_width), jnp.float32),
        compiler_params=pltpu.CompilerParams(dimension_semantics=("arbitrary",)),
    )(group_rows, group_cols, tiles, panels)


def all_reduce_by_exchange(value, axes):
    count = 1
    for axis in axes:
        count *= lax.axis_size(axis)
    rows, width = value.shape
    chunks = lax.all_to_all(value.reshape(count, rows // count, width), axes, 0, 0, tiled=True)
    own = chunks.sum(axis=0)
    spread = jnp.broadcast_to(own[None], (count,) + own.shape)
    return lax.all_to_all(spread, axes, 0, 0, tiled=True).reshape(rows, width)


def gather_by_exchange(value, axis):
    count = lax.axis_size(axis)
    copies = jnp.broadcast_to(value[None], (count,) + value.shape)
    return lax.all_to_all(copies, axis, 0, 0, tiled=True).reshape((-1,) + value.shape[1:])


def shards(features, weight, out_bias, degree, tile_row, tile_col, tile_value, cotangent):
    tile_size = tile_value.shape[1]
    nodes_dev = features.shape[0]
    block_count = nodes_dev // tile_size
    rep_count = lax.axis_size("rep")
    row_scale = lax.rsqrt(degree.astype(jnp.float32))[:, None]
    scaled = (jnp.dot(features, weight, preferred_element_type=jnp.float32) * row_scale).astype(
        jnp.bfloat16
    )
    panels = lax.all_gather(scaled, "rows", axis=0, tiled=True)
    slab_features = gather_by_exchange(features, "rep")
    slab_scale = gather_by_exchange(row_scale, "rep")
    panels, slab_features, slab_scale = lax.optimization_barrier((panels, slab_features, slab_scale))
    slab_part = aggregate_slots(panels, tile_row, tile_col, tile_value, rep_count * block_count)
    aggregate = lax.psum_scatter(slab_part, "rep", scatter_dimension=0, tiled=True) * row_scale
    pre_act = aggregate + out_bias
    hidden_out = jax.nn.silu(pre_act).astype(jnp.bfloat16)
    sigmoid_pre = jax.nn.sigmoid(pre_act)
    grad_pre = cotangent.astype(jnp.float32) * sigmoid_pre * (1.0 + pre_act * (1.0 - sigmoid_pre))
    scaled_grad = (grad_pre * row_scale).astype(jnp.bfloat16)
    grad_panels = lax.all_gather(scaled_grad, "rows", axis=0, tiled=True)
    back_part = aggregate_slots(grad_panels, tile_row, tile_col, tile_value, rep_count * block_count)
    back_total = lax.psum_scatter(back_part, "rep", scatter_dimension=0, tiled=True)
    back_sum = (back_total * row_scale).astype(jnp.bfloat16)
    grad_input = lax.dot_general(
        back_sum, weight, (((1,), (1,)), ((), ())), preferred_element_type=jnp.float32
    ).astype(jnp.bfloat16)
    local_weight = lax.dot_general(
        slab_features, back_part * slab_scale, (((0,), (0,)), ((), ())), preferred_element_type=jnp.float32
    )
    grad_weight = all_reduce_by_exchange(local_weight, ("rows", "rep"))
    return (hidden_out, grad_input, grad_weight)


def solution(mesh):
    placed = (
        P(("rows", "rep"), None),
        P(),
        P(),
        P(("rows", "rep")),
        P(("rows", "rep")),
        P(("rows", "rep")),
        P(("rows", "rep"), None, None),
        P(("rows", "rep"), None),
    )
    return jax.shard_map(
        shards,
        mesh=mesh,
        in_specs=placed,
        out_specs=(P(("rows", "rep"), None), P(("rows", "rep"), None), P()),
        check_vma=False,
    )
```
